32 devices in a mesh: dp: 8 (over z, y), tensor: 4 (over x, core).
Axes of the slice: x: 2, y: 2, z: 4, core: 2. Of those that a mesh axis runs over, the one named last changes fastest.
Arguments:
- hidden: bfloat16 [4096, 4096], P('dp'), may hold values from -40 to 40
- q_weight: bfloat16 [8192, 1024], P('dp', 'tensor'), may hold values from -0.09375 to 0.09375
- kv_weight: bfloat16 [8192, 512], P('dp', 'tensor'), may hold values from -0.09375 to 0.09375
- owner: int32 [4], replicated, may hold values from 0 to 1
- lengths: int32 [16], P('dp'), may hold values from 64 to 256, as said below
Outputs:
- attended: bfloat16 [4096, 1024], P('dp', 'tensor')
The draws below stay inside these ranges and needn't reach their ends.
Inputs may be any that keep to these rules, and one draw needn't show every extreme that they name: `lengths`: some sequence has length exactly 256.
All inputs are finite; a program needn't handle non-finite values.
Results may differ from the reference program's by a relative error of at most 0.0092.
Values may be sent and summed in bfloat16 or wider, within the bound.
No kernel may reach another device: no remote copies, remote signals or barrier semaphores. Data moves between devices by JAX's collectives and lax.ppermute only.
A program may use at most 64 MiB of HBM per device.

```python
import math
import jax
import jax.numpy as jnp
from jax import lax

D = 4096
HEAD_DIM = 128
GROUP = 4
SEQ_LEN = 256
OLD_DATA = 4
Q_HEADS = 8
KV_HEADS = 2
SECTIONS = 2
TOTAL_SEQS = 16
TOKENS = 4096


def draw_hidden(key, part):
    base_key = jax.random.fold_in(key, 0)
    values = jnp.clip(jax.random.normal(base_key, (TOKENS, D), jnp.float32), -6.0, 6.0)
    return values.astype(jnp.bfloat16)


def draw_lengths(key, part):
    first_key, second_key = jax.random.split(jax.random.fold_in(key, 11))
    values = jax.random.randint(first_key, (TOTAL_SEQS,), SEQ_LEN // 4, SEQ_LEN + 1)
    chosen = jax.random.randint(second_key, (), 0, TOTAL_SEQS)
    return values.at[chosen].set(SEQ_LEN).astype(jnp.int32)


def plant(drawn, key, low, top_value):
    spot = [jax.random.randint(jax.random.fold_in(key, axis), (), 0, length) for axis, length in enumerate(drawn.shape)]
    main_axis = drawn.shape.index(max(drawn.shape))
    neighbour = spot[:main_axis] + [(spot[main_axis] + 1) % drawn.shape[main_axis]] + spot[main_axis + 1:]
    return drawn.at[tuple(spot)].set(low).at[tuple(neighbour)].set(top_value)


def levels(stream_key, extent, pieces, low, largest):
    def one(axis_at, blocks):
        steps = jax.random.uniform(jax.random.fold_in(jax.random.fold_in(stream_key, 6), axis_at), (blocks,), jnp.float32, low / len(pieces), largest / len(pieces))
        return jnp.repeat(jnp.exp(steps), extent[axis_at] // blocks).reshape((-1,) + (1,) * (len(extent) - axis_at - 1))

    factor_of = one(*pieces[0])
    for cut in pieces[1:]:
        factor_of = factor_of * one(*cut)
    return factor_of


def bell_draw(stream_key, extent, deviation, reach, cuts=(), held_as=jnp.bfloat16):
    entries = deviation * jax.random.normal(stream_key, extent, jnp.float32)
    if cuts:
        entries = entries * levels(stream_key, extent, cuts, -0.22, 0.18)
    return jnp.clip(entries, -reach, reach).astype(held_as)


def setup_inputs(seed: int = 0) -> dict:
    key_of = jax.random.split(jax.random.key(seed), 6)
    return {
        "hidden": draw_hidden(jax.random.fold_in(key_of[5], 71), 0),
        "q_weight": bell_draw(key_of[1], (SECTIONS * D, Q_HEADS * HEAD_DIM), D ** -0.5, 0.09375, ((0, 8), (1, 4))),
        "kv_weight": bell_draw(key_of[2], (SECTIONS * D, 2 * KV_HEADS * HEAD_DIM), D ** -0.5, 0.09375, ((0, 8), (1, 4))),
        "owner": plant(jax.random.randint(key_of[3], (OLD_DATA,), 0, SECTIONS), jax.random.fold_in(key_of[3], 1), 0, SECTIONS - 1).astype(jnp.int32),
        "lengths": draw_lengths(jax.random.fold_in(key_of[5], 71), 0),
    }


def rotate(values, positions, columns, active):
    pair_index = columns % HEAD_DIM // 2
    inverse = jnp.exp(-(2.0 * pair_index.astype(jnp.float32) / HEAD_DIM) * math.log(10000.0))
    angles = positions.astype(jnp.float32)[:, None] * inverse[None, :]
    signs = jnp.where(columns % 2 == 0, -1.0, 1.0).astype(jnp.float32)
    swapped = values.reshape(values.shape[0], -1, 2)[:, :, ::-1].reshape(values.shape)
    turned = values * jnp.cos(angles) + swapped * (jnp.sin(angles) * signs[None, :])
    return jnp.where(active[None, :], turned, values)

def reference(hidden, q_weight, kv_weight, owner, lengths):
    block = D // OLD_DATA
    q_parts = []
    kv_parts = []
    for quarter in range(OLD_DATA):
        start = (owner[quarter] * D + quarter * block).astype(jnp.int32)
        q_parts.append(lax.dynamic_slice_in_dim(q_weight, start, block, 0))
        kv_parts.append(lax.dynamic_slice_in_dim(kv_weight, start, block, 0))
    w_query = jnp.concatenate(q_parts, axis=0)
    w_keyval = jnp.concatenate(kv_parts, axis=0)
    queries = jnp.dot(hidden, w_query, preferred_element_type=jnp.float32)
    keyvals = jnp.dot(hidden, w_keyval, preferred_element_type=jnp.float32)
    positions = (jnp.arange(TOKENS) % SEQ_LEN).astype(jnp.int32)
    q_columns = jnp.arange(Q_HEADS * HEAD_DIM).astype(jnp.int32)
    queries = rotate(queries, positions, q_columns, q_columns >= 0).astype(jnp.bfloat16)
    kv_columns = jnp.arange(2 * KV_HEADS * HEAD_DIM).astype(jnp.int32)
    keyvals = rotate(keyvals, positions, kv_columns, kv_columns // HEAD_DIM % 2 == 0).astype(jnp.bfloat16)
    count = TOKENS // SEQ_LEN
    q_all = queries.reshape(count, SEQ_LEN, Q_HEADS, HEAD_DIM)
    paired = keyvals.reshape(count, SEQ_LEN, KV_HEADS, 2, HEAD_DIM)
    k_all = paired[:, :, :, 0, :]
    v_all = paired[:, :, :, 1, :]
    spots = jnp.arange(SEQ_LEN).astype(jnp.int32)

    def one_sequence(item):
        q_seq, k_seq, v_seq, length = item
        k_wide = jnp.repeat(k_seq, GROUP, axis=1)
        v_wide = jnp.repeat(v_seq, GROUP, axis=1)
        scores = jnp.einsum('qhd,khd->hqk', q_seq.astype(jnp.float32), k_wide.astype(jnp.float32)) / math.sqrt(HEAD_DIM)
        allowed = (spots[None, :] <= spots[:, None]) & (spots[None, :] < length)
        scores = jnp.where(allowed[None, :, :], scores, -1e+30)
        row_max = lax.optimization_barrier(jnp.max(scores, axis=-1, keepdims=True))
        raised = jnp.exp(scores - row_max)
        row_total = lax.optimization_barrier(jnp.sum(raised, axis=-1, keepdims=True))
        probs = (raised / row_total).astype(jnp.bfloat16)
        result = jnp.einsum('hqk,khd->qhd', probs.astype(jnp.float32), v_wide.astype(jnp.float32))
        return result.astype(jnp.bfloat16).reshape(SEQ_LEN, Q_HEADS * HEAD_DIM)
    attended = lax.map(one_sequence, (q_all, k_all, v_all, lengths))
    return attended.reshape(TOKENS, Q_HEADS * HEAD_DIM)
```

```python
import math

import jax
import jax.numpy as jnp
from jax import lax
from jax.experimental import pallas as pl
from jax.experimental.pallas import tpu as pltpu
from jax.sharding import PartitionSpec as P

HEAD_DIM = 128
SEQ_LEN = 256
OLD_DATA = 4
CHUNKS = 4


def swap(value, axis, mask):
    pairs = [(source, source ^ mask) for source in range(lax.axis_size(axis))]
    return lax.ppermute(value, axis, pairs)


def gather_two(q_weight, kv_weight, owner, rank, chunks):
    quarter = rank % OLD_DATA
    keep = owner[quarter] == rank // OLD_DATA
    rows = q_weight.shape[0] // chunks
    pieces = []
    for chunk in range(chunks):
        cut = slice(chunk * rows, (chunk + 1) * rows)
        raw = jnp.concatenate([q_weight[cut], kv_weight[cut]], axis=1)
        other = swap(raw, "dp", OLD_DATA)
        mine = jnp.where(keep, raw, other)
        far = swap(mine, "dp", 2)
        side = swap(mine, "dp", 1)
        corner = swap(far, "dp", 1)
        pieces.append((mine, far, side, corner))
    order = jnp.stack([quarter, quarter ^ 2, quarter ^ 1, quarter ^ 3])
    return pieces, order


def gather_many(q_weight, kv_weight, owner, rank, sections):
    quarter = rank % OLD_DATA
    keep = owner[quarter] == rank // OLD_DATA
    raw = jnp.concatenate([q_weight, kv_weight], axis=1)
    same = [[s * OLD_DATA + q for s in range(sections)] for q in range(OLD_DATA)]
    mine = lax.psum(jnp.where(keep, raw, jnp.zeros_like(raw)), "dp", axis_index_groups=same)
    near = [[s * OLD_DATA + q for q in range(OLD_DATA)] for s in range(sections)]
    every = lax.all_gather(mine, "dp", axis_index_groups=near)
    pieces = [tuple(every[q] for q in range(OLD_DATA))]
    return pieces, jnp.arange(OLD_DATA)


def tables(tensor_index):
    columns = jnp.arange(HEAD_DIM)
    positions = jnp.arange(SEQ_LEN)
    pair_index = columns // 2
    inverse = jnp.exp(-(2.0 * pair_index.astype(jnp.float32) / HEAD_DIM) * math.log(10000.0))
    angles = positions.astype(jnp.float32)[:, None] * inverse[None, :]
    signs = jnp.where(columns % 2 == 0, -1.0, 1.0).astype(jnp.float32)
    cosine = jnp.cos(angles)
    sine = jnp.sin(angles) * signs[None, :]
    turned = tensor_index % 2 == 0
    return cosine, sine, jnp.where(turned, cosine, 1.0), jnp.where(turned, sine, 0.0)


def dot(left, right):
    return jnp.dot(left, right, preferred_element_type=jnp.float32)


def partial_kernel(order_ref, *refs):
    held, weights = refs[:OLD_DATA], refs[OLD_DATA : 2 * OLD_DATA]
    out_ref = refs[-1]
    total = dot(held[0][...], weights[0][...])
    for h_ref, w_ref in zip(held[1:], weights[1:]):
        total += dot(h_ref[...], w_ref[...])
    if len(refs) > 2 * OLD_DATA + 1:
        total += refs[2 * OLD_DATA][...]
    out_ref[...] = total


def turn(values, cosine, sine):
    lanes = lax.broadcasted_iota(jnp.int32, values.shape, 1)
    swapped = jnp.where(
        lanes % 2 == 0,
        pltpu.roll(values, values.shape[1] - 1, axis=1),
        pltpu.roll(values, 1, axis=1),
    )
    return values * cosine + swapped * sine


def last_kernel(order_ref, *refs):
    held, weights = refs[:OLD_DATA], refs[OLD_DATA : 2 * OLD_DATA]
    cos_ref, sin_ref = refs[2 * OLD_DATA], refs[2 * OLD_DATA + 1]
    out_ref = refs[-1]
    total = dot(held[0][...], weights[0][...])
    for h_ref, w_ref in zip(held[1:], weights[1:]):
        total += dot(h_ref[...], w_ref[...])
    if len(refs) > 2 * OLD_DATA + 3:
        total += refs[2 * OLD_DATA + 2][...]
    cosine, sine = cos_ref[...], sin_ref[...]
    for seq in range(total.shape[0] // SEQ_LEN):
        for head in range(total.shape[1] // HEAD_DIM):
            part = total[seq * SEQ_LEN : (seq + 1) * SEQ_LEN, head * HEAD_DIM : (head + 1) * HEAD_DIM]
            out_ref[seq * SEQ_LEN : (seq + 1) * SEQ_LEN, head * HEAD_DIM : (head + 1) * HEAD_DIM] = turn(
                part, cosine, sine
            ).astype(out_ref.dtype)


def project(kernel, order, hidden, pieces, chunk, column, width, extra, total, out_dtype):
    tokens, rows = hidden.shape[0], pieces[0].shape[0]
    chunks = hidden.shape[1] // OLD_DATA // rows

    def held(which):
        return pl.BlockSpec((tokens, rows), lambda i, order: (0, order[which] * chunks + chunk))

    in_specs = [held(which) for which in range(OLD_DATA)]
    in_specs += [pl.BlockSpec((rows, width), lambda i, order: (0, column // width))] * OLD_DATA
    in_specs += [pl.BlockSpec(value.shape, lambda i, order: (0, 0)) for value in extra]
    operands = [hidden] * OLD_DATA + list(pieces) + list(extra)
    if total is not None:
        in_specs.append(pl.BlockSpec((tokens, width), lambda i, order: (0, column // width)))
        operands.append(total)
    flops = 2 * tokens * rows * OLD_DATA * width
    moved = 2 * OLD_DATA * rows * (tokens + width) + 8 * tokens * width
    return pl.pallas_call(
        kernel,
        out_shape=jax.ShapeDtypeStruct((tokens, width), out_dtype),
        grid_spec=pltpu.PrefetchScalarGridSpec(
            num_scalar_prefetch=1,
            grid=(1,),
            in_specs=in_specs,
            out_specs=pl.BlockSpec((tokens, width), lambda i, order: (0, 0)),
        ),
        cost_estimate=pl.CostEstimate(flops=flops, bytes_accessed=moved, transcendentals=0),
    )(order, *operands)


def attend_kernel(lengths_ref, even_ref, q_ref, own_ref, partner_ref, out_ref):
    is_even = even_ref[0] == 1
    rows = lax.broadcasted_iota(jnp.int32, (SEQ_LEN, SEQ_LEN), 0)
    spots = lax.broadcasted_iota(jnp.int32, (SEQ_LEN, SEQ_LEN), 1)
    for seq in range(q_ref.shape[0] // SEQ_LEN):
        cut = slice(seq * SEQ_LEN, (seq + 1) * SEQ_LEN)
        own, partner = own_ref[cut, :], partner_ref[cut, :]
        keys = jnp.where(is_even, own, partner)
        values = jnp.where(is_even, partner, own)
        allowed = (spots <= rows) & (spots < lengths_ref[seq])
        for head in range(q_ref.shape[1] // HEAD_DIM):
            at = slice(head * HEAD_DIM, (head + 1) * HEAD_DIM)
            scores = lax.dot_general(
                q_ref[cut, at], keys, (((1,), (1,)), ((), ())), preferred_element_type=jnp.float32
            ) / math.sqrt(HEAD_DIM)
            scores = jnp.where(allowed, scores, -1e30)
            raised = jnp.exp(scores - jnp.max(scores, axis=-1, keepdims=True))
            probs = (raised / jnp.sum(raised, axis=-1, keepdims=True)).astype(jnp.bfloat16)
            out_ref[cut, at] = dot(probs, values).astype(out_ref.dtype)


def attend(lengths, even, queries, own, partner):
    whole = pl.BlockSpec(memory_space=pltpu.VMEM)
    scalar = pl.BlockSpec(memory_space=pltpu.SMEM)
    return pl.pallas_call(
        attend_kernel,
        out_shape=jax.ShapeDtypeStruct(queries.shape, jnp.bfloat16),
        in_specs=[scalar, scalar, whole, whole, whole],
        out_specs=whole,
    )(lengths, even, queries, own, partner)


def body(hidden, q_weight, kv_weight, owner, lengths):
    rank = lax.axis_index("dp")
    tensor_index = lax.axis_index("tensor")
    sections = lax.axis_size("dp") // OLD_DATA
    if sections == 2:
        pieces, order = gather_two(q_weight, kv_weight, owner, rank, CHUNKS)
    else:
        pieces, order = gather_many(q_weight, kv_weight, owner, rank, sections)
    order = order.astype(jnp.int32)
    cosine, sine, key_cosine, key_sine = tables(tensor_index)
    q_width, kv_width = q_weight.shape[1], kv_weight.shape[1]
    total = None
    for chunk, held in enumerate(pieces[:-1]):
        total = project(
            partial_kernel, order, hidden, held, chunk, 0, q_width + kv_width, [], total, jnp.float32
        )
    last = len(pieces) - 1
    own = project(
        last_kernel, order, hidden, pieces[-1], last, q_width, kv_width, [key_cosine, key_sine], total, jnp.bfloat16
    )
    partner = swap(own, "tensor", 1)
    queries = project(
        last_kernel, order, hidden, pieces[-1], last, 0, q_width, [cosine, sine], total, jnp.bfloat16
    )
    even = (tensor_index % 2 == 0).astype(jnp.int32).reshape(1)
    return attend(lengths, even, queries, own, partner)


def solution(mesh):
    return jax.shard_map(
        body,
        mesh=mesh,
        in_specs=(P("dp", None), P("dp", "tensor"), P("dp", "tensor"), P(), P("dp")),
        out_specs=P("dp", "tensor"),
        check_vma=False,
    )
```

```python
import functools
import math

import jax
import jax.numpy as jnp
from jax import lax
from jax.experimental import pallas as pl
from jax.experimental.pallas import tpu as pltpu
from jax.sharding import PartitionSpec as P


HEAD_DIM = 128
SEQ_LEN = 256
OLD_DATA = 4
IN_FLIGHT = 2


VMEM = pl.BlockSpec(memory_space=pltpu.VMEM)
SMEM = pl.BlockSpec(memory_space=pltpu.SMEM)


def swapped(value, axis, mask):
    pairs = [(source, source ^ mask) for source in range(lax.axis_size(axis))]
    return lax.ppermute(value, axis, pairs)


def near(value):
    return pltpu.with_memory_space_constraint(value, pltpu.VMEM)


def dot(left, right):
    return jnp.dot(left, right, preferred_element_type=jnp.float32)


def call(kernel, scalars, operands, outs, cost, out_specs=VMEM, spare=(), **more):
    return pl.pallas_call(
        kernel,
        out_shape=outs,
        in_specs=[SMEM] * len(scalars)
        + [VMEM] * len(operands)
        + [pl.BlockSpec(memory_space=pltpu.HBM)] * len(spare),
        out_specs=jax.tree.map(lambda _: out_specs, outs),
        compiler_params=pltpu.CompilerParams(vmem_limit_bytes=8 * 2**20),
        cost_estimate=pl.CostEstimate(flops=cost, bytes_accessed=cost // 256, transcendentals=0),
        **more,
    )(*scalars, *operands, *spare)


def tables(turned):
    columns = jnp.arange(HEAD_DIM)
    positions = jnp.arange(SEQ_LEN)
    pair_index = columns // 2
    inverse = jnp.exp(-(2.0 * pair_index.astype(jnp.float32) / HEAD_DIM) * math.log(10000.0))
    angles = positions.astype(jnp.float32)[:, None] * inverse[None, :]
    signs = jnp.where(columns % 2 == 0, -1.0, 1.0).astype(jnp.float32)
    cosine = jnp.cos(angles)
    sine = jnp.sin(angles) * signs[None, :]
    return cosine, sine, jnp.where(turned, cosine, 1.0), jnp.where(turned, sine, 0.0)


def turn(values, cosine, sine):
    lanes = lax.broadcasted_iota(jnp.int32, values.shape, 1)
    swapped = jnp.where(
        lanes % 2 == 0,
        pltpu.roll(values, values.shape[1] - 1, axis=1),
        pltpu.roll(values, 1, axis=1),
    )
    return values * cosine + swapped * sine


def attend_head(queries, keys, values, length):
    half = SEQ_LEN // 2
    scale = math.log2(math.e) / math.sqrt(HEAD_DIM)
    parts = []
    for start, stop in ((0, half), (half, SEQ_LEN)):
        rows = start + lax.broadcasted_iota(jnp.int32, (stop - start, stop), 0)
        spots = lax.broadcasted_iota(jnp.int32, (stop - start, stop), 1)
        scores = lax.dot_general(
            queries[start:stop], keys[:stop], (((1,), (1,)), ((), ())), preferred_element_type=jnp.float32
        )
        scores = jnp.where((spots <= rows) & (spots < length), scores, -1e30)
        top = jnp.max(scores, axis=-1, keepdims=True)
        raised = jnp.exp2((scores - top) * scale)
        total = jnp.sum(raised, axis=-1, keepdims=True)
        parts.append(dot(raised.astype(jnp.bfloat16), values[:stop]) / total)
    return jnp.concatenate(parts, axis=0)


def choose_kernel(keep_ref, raw_ref, other_ref, out_ref):
    @pl.when(keep_ref[0] == 1)
    def _():
        out_ref[...] = raw_ref[...]

    @pl.when(keep_ref[0] != 1)
    def _():
        out_ref[...] = other_ref[...]


def choose(keep, raw, other):
    return call(choose_kernel, [keep], [near(raw), near(other)], pltpu.VMEM(raw.shape, raw.dtype), raw.size)


def own_kernel(own_ref, mine_ref, far_ref, out_ref):
    depth = mine_ref.shape[0]
    out_ref[...] = dot(own_ref[:, :depth], mine_ref[...]) + dot(own_ref[:, depth:], far_ref[...])


def their_kernel(core_ref, first_ref, second_ref, mine_ref, far_ref, out_ref):
    half, depth = first_ref.shape[0], mine_ref.shape[0]
    mine, far = mine_ref[...], far_ref[...]
    for which, ref in ((core_ref[0], first_ref), (1 - core_ref[0], second_ref)):
        total = dot(ref[:, :depth], mine) + dot(ref[:, depth:], far)
        out_ref[pl.ds(pl.multiple_of(which * half, half), half), :] = total.astype(out_ref.dtype)


def finish_kernel(own_ref, sent_ref, cos_ref, sin_ref, out_ref):
    for seq in range(own_ref.shape[0] // SEQ_LEN):
        cut = slice(seq * SEQ_LEN, (seq + 1) * SEQ_LEN)
        total = own_ref[cut, :] + sent_ref[cut, :].astype(jnp.float32)
        out_ref[cut, :] = turn(total, cos_ref[...], sin_ref[...]).astype(out_ref.dtype)


def head_kernel(head, lengths_ref, even_ref, own_ref, sent_ref, cos_ref, sin_ref, kv_ref, partner_ref, *refs):
    is_even = even_ref[0] == 1
    out_ref, held, sems = refs[-3:]
    columns = slice(head * HEAD_DIM, (head + 1) * HEAD_DIM)
    copies = []
    for seq in range(own_ref.shape[0] // SEQ_LEN):
        cut = slice(seq * SEQ_LEN, (seq + 1) * SEQ_LEN)
        total = own_ref[cut, :] + sent_ref[cut, :].astype(jnp.float32)
        queries = turn(total, cos_ref[...], sin_ref[...]).astype(jnp.bfloat16)
        mine, partner = kv_ref[cut, :], partner_ref[cut, :]
        keys = jnp.where(is_even, mine, partner)
        values = jnp.where(is_even, partner, mine)
        held[cut, :] = attend_head(queries, keys, values, lengths_ref[seq]).astype(held.dtype)
        copies.append(pltpu.make_async_copy(held.at[cut, :], out_ref.at[cut, columns], sems.at[seq]))
        copies[-1].start()
    for copy in copies:
        copy.wait()


def two_sections(hidden, q_weight, kv_weight, owner, lengths):
    rank, tensor_index = lax.axis_index("dp"), lax.axis_index("tensor")
    quarter, core = rank % OLD_DATA, tensor_index % 2
    keep = owner[quarter] == rank // OLD_DATA
    depth, tokens = q_weight.shape[0], hidden.shape[0]
    heads = q_weight.shape[1] // HEAD_DIM
    after = lax.optimization_barrier

    half = tokens // 2
    given = lambda w: lax.dynamic_slice(hidden, (core * half, w * depth), (half, depth))
    sent = jnp.concatenate([given(quarter ^ 1), given(quarter ^ 3)], axis=1)
    whole = lambda w: lax.dynamic_slice(hidden, (0, w * depth), (tokens, depth))
    own_part = jnp.concatenate([whole(quarter), whole(quarter ^ 2)], axis=1)
    first = swapped(sent, "dp", 1)

    columns = [q_weight[:, head * HEAD_DIM : (head + 1) * HEAD_DIM] for head in range(heads)]
    blocks = [kv_weight, *after(tuple(columns))]
    others = []
    for index, raw in enumerate(blocks):
        if index >= IN_FLIGHT:
            raw, others[index - IN_FLIGHT] = after((raw, others[index - IN_FLIGHT]))
        blocks[index] = raw
        others.append(swapped(raw, "dp", OLD_DATA))
    even = (core == 0).astype(jnp.int32).reshape(1)
    core = core.astype(jnp.int32).reshape(1)
    keep = keep.astype(jnp.int32).reshape(1)
    first, turns = after((first, tables(even[0] == 1)))
    cosine, sine, key_cosine, key_sine = turns
    second = swapped(first, "tensor", 1)
    settled = []
    for raw, other in zip(blocks, others):
        mine = choose(keep, raw, other)
        settled.append((mine, swapped(mine, "dp", 2)))

    own_kv = partner = result = None
    work = 4 * tokens * depth * HEAD_DIM
    for index, (mine, far) in enumerate(settled):
        theirs = call(
            their_kernel,
            [core],
            [near(value) for value in (first, second, mine, far)],
            pltpu.VMEM((tokens, HEAD_DIM), jnp.bfloat16),
            work,
        )
        back = swapped(theirs, "dp", 1)
        own = call(
            own_kernel,
            [],
            [near(value) for value in (own_part, mine, far)],
            pltpu.VMEM((tokens, HEAD_DIM), jnp.float32),
            work,
        )
        if index == 0:
            own_kv = call(
                finish_kernel,
                [],
                [near(value) for value in (own, back, key_cosine, key_sine)],
                pltpu.VMEM((tokens, HEAD_DIM), jnp.bfloat16),
                tokens * HEAD_DIM * 8,
            )
            partner = swapped(own_kv, "tensor", 1)
            continue
        head = index - 1
        result = call(
            functools.partial(head_kernel, head),
            [lengths, even],
            [near(value) for value in (own, back, cosine, sine, own_kv, partner)],
            jax.ShapeDtypeStruct((tokens, heads * HEAD_DIM), jnp.bfloat16),
            tokens * SEQ_LEN * HEAD_DIM * 4,
            out_specs=pl.BlockSpec(memory_space=pltpu.HBM),
            scratch_shapes=[
                pltpu.VMEM((tokens, HEAD_DIM), jnp.bfloat16),
                pltpu.SemaphoreType.DMA((tokens // SEQ_LEN,)),
            ],
            spare=[] if result is None else [result],
            input_output_aliases={} if result is None else {8: 0},
        )
    return result


def many_sections(hidden, q_weight, kv_weight, owner, lengths):
    rank, tensor_index = lax.axis_index("dp"), lax.axis_index("tensor")
    sections = lax.axis_size("dp") // OLD_DATA
    quarter, core = rank % OLD_DATA, tensor_index % 2
    keep = owner[quarter] == rank // OLD_DATA
    raw = jnp.concatenate([q_weight, kv_weight], axis=1)
    same = [[s * OLD_DATA + q for s in range(sections)] for q in range(OLD_DATA)]
    mine = lax.psum(jnp.where(keep, raw, jnp.zeros_like(raw)), "dp", axis_index_groups=same)
    group = [[s * OLD_DATA + q for q in range(OLD_DATA)] for s in range(sections)]
    weight = lax.all_gather(mine, "dp", axis_index_groups=group, tiled=True)
    q_width, tokens = q_weight.shape[1], hidden.shape[0]
    seqs = tokens // SEQ_LEN
    cosine, sine, key_cosine, key_sine = tables(core == 0)

    def turned(values, cosine, sine):
        shaped = values.reshape(seqs, SEQ_LEN, -1, HEAD_DIM // 2, 2)
        swapped = shaped[..., ::-1].reshape(seqs, SEQ_LEN, -1, HEAD_DIM)
        straight = values.reshape(seqs, SEQ_LEN, -1, HEAD_DIM)
        return (straight * cosine[:, None, :] + swapped * sine[:, None, :]).astype(jnp.bfloat16)

    queries = turned(dot(hidden, weight[:, :q_width]), cosine, sine)
    own = turned(dot(hidden, weight[:, q_width:]), key_cosine, key_sine)[:, :, 0]
    partner = swapped(own, "tensor", 1)
    keys = jnp.where(core == 0, own, partner)
    values = jnp.where(core == 0, partner, own)
    spots = jnp.arange(SEQ_LEN)
    allowed = (spots[None, None, :] <= spots[None, :, None]) & (spots[None, None, :] < lengths[:, None, None])
    scores = jnp.einsum("sqhd,skd->shqk", queries, keys, preferred_element_type=jnp.float32)
    scores = jnp.where(allowed[:, None], scores / math.sqrt(HEAD_DIM), -1e30)
    raised = jnp.exp(scores - jnp.max(scores, axis=-1, keepdims=True))
    probs = (raised / jnp.sum(raised, axis=-1, keepdims=True)).astype(jnp.bfloat16)
    mixed = jnp.einsum("shqk,skd->sqhd", probs, values, preferred_element_type=jnp.float32)
    return mixed.astype(jnp.bfloat16).reshape(tokens, q_width)


def body(hidden, q_weight, kv_weight, owner, lengths):
    if lax.axis_size("dp") == 2 * OLD_DATA:
        return two_sections(hidden, q_weight, kv_weight, owner, lengths)
    return many_sections(hidden, q_weight, kv_weight, owner, lengths)


def solution(mesh):
    return jax.shard_map(
        body,
        mesh=mesh,
        in_specs=(P("dp", None), P("dp", "tensor"), P("dp", "tensor"), P(), P("dp")),
        out_specs=P("dp", "tensor"),
        check_vma=False,
    )
```

```python
import functools
import math

import jax
import jax.numpy as jnp
from jax import lax
from jax.experimental import pallas as pl
from jax.experimental.pallas import tpu as pltpu
from jax.sharding import PartitionSpec as P


HEAD_DIM = 128
SEQ_LEN = 256
OLD_DATA = 4
IN_FLIGHT = 2


VMEM = pl.BlockSpec(memory_space=pltpu.VMEM)
SMEM = pl.BlockSpec(memory_space=pltpu.SMEM)
ANY = pl.BlockSpec(memory_space=pl.ANY)


def swapped(value, axis, mask):
    pairs = [(source, source ^ mask) for source in range(lax.axis_size(axis))]
    return lax.ppermute(value, axis, pairs)


def near(value):
    return pltpu.with_memory_space_constraint(value, pltpu.VMEM)


def dot(left, right):
    return jnp.dot(left, right, preferred_element_type=jnp.float32)


def call(kernel, scalars, operands, outs, cost, out_specs=VMEM, spare=(), **more):
    return pl.pallas_call(
        kernel,
        out_shape=outs,
        in_specs=[SMEM] * len(scalars)
        + [VMEM] * len(operands)
        + [pl.BlockSpec(memory_space=pltpu.HBM)] * len(spare),
        out_specs=jax.tree.map(lambda _: out_specs, outs),
        compiler_params=pltpu.CompilerParams(vmem_limit_bytes=8 * 2**20),
        cost_estimate=pl.CostEstimate(flops=cost, bytes_accessed=cost // 256, transcendentals=0),
        **more,
    )(*scalars, *operands, *spare)


def tables(turned):
    columns = jnp.arange(HEAD_DIM)
    positions = jnp.arange(SEQ_LEN)
    pair_index = columns // 2
    inverse = jnp.exp(-(2.0 * pair_index.astype(jnp.float32) / HEAD_DIM) * math.log(10000.0))
    angles = positions.astype(jnp.float32)[:, None] * inverse[None, :]
    signs = jnp.where(columns % 2 == 0, -1.0, 1.0).astype(jnp.float32)
    cosine = jnp.cos(angles)
    sine = jnp.sin(angles) * signs[None, :]
    return cosine, sine, jnp.where(turned, cosine, 1.0), jnp.where(turned, sine, 0.0)


def turn(values, cosine, sine):
    lanes = lax.broadcasted_iota(jnp.int32, values.shape, 1)
    swapped = jnp.where(
        lanes % 2 == 0,
        pltpu.roll(values, values.shape[1] - 1, axis=1),
        pltpu.roll(values, 1, axis=1),
    )
    return values * cosine + swapped * sine


def attend_head(queries, keys, values, length):
    half = SEQ_LEN // 2
    scale = math.log2(math.e) / math.sqrt(HEAD_DIM)
    parts = []
    for start, stop in ((0, half), (half, SEQ_LEN)):
        rows = start + lax.broadcasted_iota(jnp.int32, (stop - start, stop), 0)
        spots = lax.broadcasted_iota(jnp.int32, (stop - start, stop), 1)
        scores = lax.dot_general(
            queries[start:stop], keys[:stop], (((1,), (1,)), ((), ())), preferred_element_type=jnp.float32
        )
        scores = jnp.where((spots <= rows) & (spots < length), scores, -1e30)
        top = jnp.max(scores, axis=-1, keepdims=True)
        raised = jnp.exp2((scores - top) * scale)
        total = jnp.sum(raised, axis=-1, keepdims=True)
        parts.append(dot(raised.astype(jnp.bfloat16), values[:stop]) / total)
    return jnp.concatenate(parts, axis=0)


def choose_kernel(keep_ref, raw_ref, other_ref, out_ref, sem):
    for kept, ref in ((1, raw_ref), (0, other_ref)):

        @pl.when(keep_ref[0] == kept)
        def _(ref=ref):
            copy = pltpu.make_async_copy(ref, out_ref, sem)
            copy.start()
            copy.wait()


def choose(keep, raw, other):
    return pl.pallas_call(
        choose_kernel,
        out_shape=pltpu.VMEM(raw.shape, raw.dtype),
        in_specs=[SMEM, ANY, ANY],
        out_specs=VMEM,
        scratch_shapes=[pltpu.SemaphoreType.DMA],
        compiler_params=pltpu.CompilerParams(vmem_limit_bytes=8 * 2**20),
        cost_estimate=pl.CostEstimate(flops=0, bytes_accessed=4 * raw.size, transcendentals=0),
    )(keep, raw, other)


def own_kernel(own_ref, mine_ref, far_ref, out_ref):
    depth = mine_ref.shape[0]
    out_ref[...] = dot(own_ref[:, :depth], mine_ref[...]) + dot(own_ref[:, depth:], far_ref[...])


def their_kernel(core_ref, first_ref, second_ref, mine_ref, far_ref, out_ref):
    half, depth = first_ref.shape[0], mine_ref.shape[0]
    mine, far = mine_ref[...], far_ref[...]
    for which, ref in ((core_ref[0], first_ref), (1 - core_ref[0], second_ref)):
        total = dot(ref[:, :depth], mine) + dot(ref[:, depth:], far)
        out_ref[pl.ds(pl.multiple_of(which * half, half), half), :] = total.astype(out_ref.dtype)


def finish_kernel(own_ref, sent_ref, cos_ref, sin_ref, out_ref):
    for seq in range(own_ref.shape[0] // SEQ_LEN):
        cut = slice(seq * SEQ_LEN, (seq + 1) * SEQ_LEN)
        total = own_ref[cut, :] + sent_ref[cut, :].astype(jnp.float32)
        out_ref[cut, :] = turn(total, cos_ref[...], sin_ref[...]).astype(out_ref.dtype)


def head_kernel(head, lengths_ref, even_ref, own_ref, sent_ref, cos_ref, sin_ref, kv_ref, partner_ref, *refs):
    is_even = even_ref[0] == 1
    out_ref, held, sems = refs[-3:]
    columns = slice(head * HEAD_DIM, (head + 1) * HEAD_DIM)
    copies = []
    for seq in range(own_ref.shape[0] // SEQ_LEN):
        cut = slice(seq * SEQ_LEN, (seq + 1) * SEQ_LEN)
        total = own_ref[cut, :] + sent_ref[cut, :].astype(jnp.float32)
        queries = turn(total, cos_ref[...], sin_ref[...]).astype(jnp.bfloat16)
        mine, partner = kv_ref[cut, :], partner_ref[cut, :]
        keys = jnp.where(is_even, mine, partner)
        values = jnp.where(is_even, partner, mine)
        held[cut, :] = attend_head(queries, keys, values, lengths_ref[seq]).astype(held.dtype)
        copies.append(pltpu.make_async_copy(held.at[cut, :], out_ref.at[cut, columns], sems.at[seq]))
        copies[-1].start()
    for copy in copies:
        copy.wait()


def two_sections(hidden, q_weight, kv_weight, owner, lengths):
    rank, tensor_index = lax.axis_index("dp"), lax.axis_index("tensor")
    quarter, core = rank % OLD_DATA, tensor_index % 2
    keep = owner[quarter] == rank // OLD_DATA
    depth, tokens = q_weight.shape[0], hidden.shape[0]
    heads = q_weight.shape[1] // HEAD_DIM
    after = lax.optimization_barrier

    half = tokens // 2
    given = lambda w: lax.dynamic_slice(hidden, (core * half, w * depth), (half, depth))
    sent = jnp.concatenate([given(quarter ^ 1), given(quarter ^ 3)], axis=1)
    whole = lambda w: lax.dynamic_slice(hidden, (0, w * depth), (tokens, depth))
    own_part = jnp.concatenate([whole(quarter), whole(quarter ^ 2)], axis=1)
    first = swapped(sent, "dp", 1)

    columns = [q_weight[:, head * HEAD_DIM : (head + 1) * HEAD_DIM] for head in range(heads)]
    blocks = [kv_weight, *after(tuple(columns))]
    others = []
    for index, raw in enumerate(blocks):
        if index >= IN_FLIGHT:
            raw, own_part = after((raw, own_part))
            raw, others[index - IN_FLIGHT] = after((raw, others[index - IN_FLIGHT]))
        blocks[index] = raw
        others.append(swapped(raw, "dp", OLD_DATA))
    even = (core == 0).astype(jnp.int32).reshape(1)
    core = core.astype(jnp.int32).reshape(1)
    keep = keep.astype(jnp.int32).reshape(1)
    first, turns = after((first, tables(even[0] == 1)))
    cosine, sine, key_cosine, key_sine = turns
    second = swapped(first, "tensor", 1)
    settled = []
    for raw, other in zip(blocks, others):
        mine = choose(keep, raw, other)
        settled.append((mine, swapped(mine, "dp", 2)))

    own_kv = partner = result = None
    work = 4 * tokens * depth * HEAD_DIM
    for index, (mine, far) in enumerate(settled):
        theirs = call(
            their_kernel,
            [core],
            [near(value) for value in (first, second, mine, far)],
            pltpu.VMEM((tokens, HEAD_DIM), jnp.bfloat16),
            work,
        )
        back = swapped(theirs, "dp", 1)
        own = call(
            own_kernel,
            [],
            [near(value) for value in (own_part, mine, far)],
            pltpu.VMEM((tokens, HEAD_DIM), jnp.float32),
            work,
        )
        if index == 0:
            own_kv = call(
                finish_kernel,
                [],
                [near(value) for value in (own, back, key_cosine, key_sine)],
                pltpu.VMEM((tokens, HEAD_DIM), jnp.bfloat16),
                tokens * HEAD_DIM * 8,
            )
            partner = swapped(own_kv, "tensor", 1)
            continue
        head = index - 1
        result = call(
            functools.partial(head_kernel, head),
            [lengths, even],
            [near(value) for value in (own, back, cosine, sine, own_kv, partner)],
            jax.ShapeDtypeStruct((tokens, heads * HEAD_DIM), jnp.bfloat16),
            tokens * SEQ_LEN * HEAD_DIM * 4,
            out_specs=pl.BlockSpec(memory_space=pltpu.HBM),
            scratch_shapes=[
                pltpu.VMEM((tokens, HEAD_DIM), jnp.bfloat16),
                pltpu.SemaphoreType.DMA((tokens // SEQ_LEN,)),
            ],
            spare=[] if result is None else [result],
            input_output_aliases={} if result is None else {8: 0},
        )
    return result


def many_sections(hidden, q_weight, kv_weight, owner, lengths):
    rank, tensor_index = lax.axis_index("dp"), lax.axis_index("tensor")
    sections = lax.axis_size("dp") // OLD_DATA
    quarter, core = rank % OLD_DATA, tensor_index % 2
    keep = owner[quarter] == rank // OLD_DATA
    raw = jnp.concatenate([q_weight, kv_weight], axis=1)
    same = [[s * OLD_DATA + q for s in range(sections)] for q in range(OLD_DATA)]
    mine = lax.psum(jnp.where(keep, raw, jnp.zeros_like(raw)), "dp", axis_index_groups=same)
    group = [[s * OLD_DATA + q for q in range(OLD_DATA)] for s in range(sections)]
    weight = lax.all_gather(mine, "dp", axis_index_groups=group, tiled=True)
    q_width, tokens = q_weight.shape[1], hidden.shape[0]
    seqs = tokens // SEQ_LEN
    cosine, sine, key_cosine, key_sine = tables(core == 0)

    def turned(values, cosine, sine):
        shaped = values.reshape(seqs, SEQ_LEN, -1, HEAD_DIM // 2, 2)
        swapped = shaped[..., ::-1].reshape(seqs, SEQ_LEN, -1, HEAD_DIM)
        straight = values.reshape(seqs, SEQ_LEN, -1, HEAD_DIM)
        return (straight * cosine[:, None, :] + swapped * sine[:, None, :]).astype(jnp.bfloat16)

    queries = turned(dot(hidden, weight[:, :q_width]), cosine, sine)
    own = turned(dot(hidden, weight[:, q_width:]), key_cosine, key_sine)[:, :, 0]
    partner = swapped(own, "tensor", 1)
    keys = jnp.where(core == 0, own, partner)
    values = jnp.where(core == 0, partner, own)
    spots = jnp.arange(SEQ_LEN)
    allowed = (spots[None, None, :] <= spots[None, :, None]) & (spots[None, None, :] < lengths[:, None, None])
    scores = jnp.einsum("sqhd,skd->shqk", queries, keys, preferred_element_type=jnp.float32)
    scores = jnp.where(allowed[:, None], scores / math.sqrt(HEAD_DIM), -1e30)
    raised = jnp.exp(scores - jnp.max(scores, axis=-1, keepdims=True))
    probs = (raised / jnp.sum(raised, axis=-1, keepdims=True)).astype(jnp.bfloat16)
    mixed = jnp.einsum("shqk,skd->sqhd", probs, values, preferred_element_type=jnp.float32)
    return mixed.astype(jnp.bfloat16).reshape(tokens, q_width)


def body(hidden, q_weight, kv_weight, owner, lengths):
    if lax.axis_size("dp") == 2 * OLD_DATA:
        return two_sections(hidden, q_weight, kv_weight, owner, lengths)
    return many_sections(hidden, q_weight, kv_weight, owner, lengths)


def solution(mesh):
    return jax.shard_map(
        body,
        mesh=mesh,
        in_specs=(P("dp", None), P("dp", "tensor"), P("dp", "tensor"), P(), P("dp")),
        out_specs=P("dp", "tensor"),
        check_vma=False,
    )
```

```python
import functools
import math

import jax
import jax.numpy as jnp
from jax import lax
from jax.experimental import pallas as pl
from jax.experimental.pallas import tpu as pltpu
from jax.sharding import PartitionSpec as P


HEAD_DIM = 128
SEQ_LEN = 256
OLD_DATA = 4


VMEM = pl.BlockSpec(memory_space=pltpu.VMEM)
SMEM = pl.BlockSpec(memory_space=pltpu.SMEM)
ANY = pl.BlockSpec(memory_space=pl.ANY)


def swapped(value, axis, mask):
    pairs = [(source, source ^ mask) for source in range(lax.axis_size(axis))]
    return lax.ppermute(value, axis, pairs)


def near(value):
    return pltpu.with_memory_space_constraint(value, pltpu.VMEM)


def dot(left, right):
    return jnp.dot(left, right, preferred_element_type=jnp.float32)


def call(kernel, scalars, operands, outs, cost, out_specs=VMEM, **more):
    return pl.pallas_call(
        kernel,
        out_shape=outs,
        in_specs=[SMEM] * len(scalars) + [VMEM] * len(operands),
        out_specs=jax.tree.map(lambda _: out_specs, outs),
        compiler_params=pltpu.CompilerParams(vmem_limit_bytes=8 * 2**20),
        cost_estimate=pl.CostEstimate(flops=cost, bytes_accessed=cost // 256, transcendentals=0),
        **more,
    )(*scalars, *operands)


def tables(turned):
    columns = jnp.arange(HEAD_DIM)
    positions = jnp.arange(SEQ_LEN)
    pair_index = columns // 2
    inverse = jnp.exp(-(2.0 * pair_index.astype(jnp.float32) / HEAD_DIM) * math.log(10000.0))
    angles = positions.astype(jnp.float32)[:, None] * inverse[None, :]
    signs = jnp.where(columns % 2 == 0, -1.0, 1.0).astype(jnp.float32)
    cosine = jnp.cos(angles)
    sine = jnp.sin(angles) * signs[None, :]
    return cosine, sine, jnp.where(turned, cosine, 1.0), jnp.where(turned, sine, 0.0)


def turn(values, cosine, sine):
    lanes = lax.broadcasted_iota(jnp.int32, values.shape, 1)
    swapped = jnp.take_along_axis(values, lanes ^ 1, axis=1, mode="promise_in_bounds")
    return values * cosine + swapped * sine


def attend_head(queries, keys, values, length):
    half = SEQ_LEN // 2
    scale = math.log2(math.e) / math.sqrt(HEAD_DIM)
    values = jnp.concatenate([values, jnp.ones_like(values)], axis=1)
    parts = []
    for start, stop in ((0, half), (half, SEQ_LEN)):
        rows = start + lax.broadcasted_iota(jnp.int32, (stop - start, stop), 0)
        spots = lax.broadcasted_iota(jnp.int32, (stop - start, stop), 1)
        scores = lax.dot_general(
            queries[start:stop], keys[:stop], (((1,), (1,)), ((), ())), preferred_element_type=jnp.float32
        )
        scores = jnp.where((spots <= rows) & (spots < length), scores, -1e30)
        top = jnp.max(scores, axis=-1, keepdims=True)
        raised = jnp.exp2((scores - top) * scale).astype(jnp.bfloat16)
        mixed = dot(raised, values[:stop])
        parts.append(mixed[:, :HEAD_DIM] / mixed[:, HEAD_DIM:])
    return jnp.concatenate(parts, axis=0)


def choose_kernel(keep_ref, raw_ref, other_ref, out_ref, sem):
    for kept, ref in ((1, raw_ref), (0, other_ref)):

        @pl.when(keep_ref[0] == kept)
        def _(ref=ref):
            copy = pltpu.make_async_copy(ref, out_ref, sem)
            copy.start()
            copy.wait()


def choose(keep, raw, other):
    return pl.pallas_call(
        choose_kernel,
        out_shape=pltpu.VMEM(raw.shape, raw.dtype),
        in_specs=[SMEM, ANY, ANY],
        out_specs=VMEM,
        scratch_shapes=[pltpu.SemaphoreType.DMA],
        compiler_params=pltpu.CompilerParams(vmem_limit_bytes=8 * 2**20),
        cost_estimate=pl.CostEstimate(flops=0, bytes_accessed=4 * raw.size, transcendentals=0),
    )(keep, raw, other)


def own_kernel(own_ref, mine_ref, far_ref, out_ref):
    depth = mine_ref.shape[0]
    out_ref[...] = dot(own_ref[:, :depth], mine_ref[...]) + dot(own_ref[:, depth:], far_ref[...])


def their_kernel(start, core_ref, first_ref, second_ref, block_ref, *refs):
    out_ref, half, depth = refs[-1], first_ref.shape[0], block_ref.shape[0]
    block = block_ref[...]
    for which, ref in ((core_ref[0], first_ref), (1 - core_ref[0], second_ref)):
        at = pl.ds(pl.multiple_of(which * half, half), half)
        total = dot(ref[:, start : start + depth], block)
        if len(refs) > 1:
            total += refs[0][at, :]
        out_ref[at, :] = total.astype(out_ref.dtype)


def finish_kernel(own_ref, sent_ref, cos_ref, sin_ref, out_ref):
    for seq in range(own_ref.shape[0] // SEQ_LEN):
        cut = slice(seq * SEQ_LEN, (seq + 1) * SEQ_LEN)
        total = own_ref[cut, :] + sent_ref[cut, :].astype(jnp.float32)
        out_ref[cut, :] = turn(total, cos_ref[...], sin_ref[...]).astype(out_ref.dtype)


def head_kernel(facts_ref, own_ref, sent_ref, cos_ref, sin_ref, kv_ref, partner_ref, *refs):
    seqs = own_ref.shape[0] // SEQ_LEN
    is_even = facts_ref[seqs] == 1
    last = len(refs) > 1
    done_refs, held = refs[:-3], refs[-2] if last else refs[0]
    copies = []

    def send(ref, head, cut):
        if last:
            columns = slice(head * HEAD_DIM, (head + 1) * HEAD_DIM)
            copy = pltpu.make_async_copy(ref.at[cut, :], refs[-3].at[cut, columns], refs[-1].at[len(copies)])
            copies.append(copy)
            copy.start()

    for head, ref in enumerate(done_refs):
        send(ref, head, slice(0, ref.shape[0]))
    for seq in range(seqs):
        cut = slice(seq * SEQ_LEN, (seq + 1) * SEQ_LEN)
        total = own_ref[cut, :] + sent_ref[cut, :].astype(jnp.float32)
        queries = turn(total, cos_ref[...], sin_ref[...]).astype(jnp.bfloat16)
        mine, partner = kv_ref[cut, :], partner_ref[cut, :]
        keys = jnp.where(is_even, mine, partner)
        values = jnp.where(is_even, partner, mine)
        held[cut, :] = attend_head(queries, keys, values, facts_ref[seq]).astype(held.dtype)
        send(held, len(done_refs), cut)
    for copy in copies:
        copy.wait()


def two_sections(hidden, q_weight, kv_weight, owner, lengths):
    rank, tensor_index = lax.axis_index("dp"), lax.axis_index("tensor")
    quarter, core = rank % OLD_DATA, tensor_index % 2
    keep = owner[quarter] == rank // OLD_DATA
    depth, tokens = q_weight.shape[0], hidden.shape[0]
    heads = q_weight.shape[1] // HEAD_DIM
    after = lax.optimization_barrier

    half = tokens // 2
    given = lambda w: lax.dynamic_slice(hidden, (core * half, w * depth), (half, depth))
    sent = jnp.concatenate([given(quarter ^ 1), given(quarter ^ 3)], axis=1)
    whole = lambda w: lax.dynamic_slice(hidden, (0, w * depth), (tokens, depth))
    own_part = jnp.concatenate([whole(quarter), whole(quarter ^ 2)], axis=1)
    first = swapped(sent, "dp", 1)

    columns = [q_weight[:, head * HEAD_DIM : (head + 1) * HEAD_DIM] for head in range(heads)]
    blocks = [kv_weight, *after(tuple(columns))]
    others = []
    for index, raw in enumerate(blocks):
        if index == 1:
            raw, staged = after((raw, choose(jnp.ones((1,), jnp.int32), kv_weight, kv_weight)))
            blocks[0] = staged
        if index:
            raw, others[0] = after((raw, others[0]))
        if index > 1:
            raw, own_part = after((raw, own_part))
        blocks[index] = raw
        others.append(swapped(raw, "dp", OLD_DATA))
    even = (core == 0).astype(jnp.int32).reshape(1)
    facts = jnp.concatenate([lengths, even])
    core = core.astype(jnp.int32).reshape(1)
    keep = keep.astype(jnp.int32).reshape(1)
    first, turns = after((first, tables(even[0] == 1)))
    cosine, sine, key_cosine, key_sine = turns
    second = swapped(first, "tensor", 1)
    settled = []
    for raw, other in zip(blocks, others):
        mine = choose(keep, raw, other)
        settled.append((mine, swapped(mine, "dp", 2)))

    sums, dots = [], 4 * tokens * depth * HEAD_DIM
    for index, (mine, far) in enumerate(settled):
        if index > 1:
            own, back = sums[-1]
            far, own = after((far, own))
            sums[-1] = (own, back)
        theirs = call(
            functools.partial(their_kernel, 0),
            [core],
            [near(value) for value in (first, second, mine)],
            pltpu.VMEM((tokens, HEAD_DIM), jnp.float32),
            dots // 2,
        )
        if index > 1:
            far, theirs = after((far, theirs))
        theirs = call(
            functools.partial(their_kernel, depth),
            [core],
            [near(value) for value in (first, second, far, theirs)],
            pltpu.VMEM((tokens, HEAD_DIM), jnp.float32 if index < 2 else jnp.bfloat16),
            dots // 2,
        )
        back = swapped(theirs, "dp", 1)
        own = call(
            own_kernel,
            [],
            [near(value) for value in (own_part, mine, far)],
            pltpu.VMEM((tokens, HEAD_DIM), jnp.float32),
            dots,
        )
        sums.append((own, back))
        if index == 0:
            own_kv = call(
                finish_kernel,
                [],
                [near(value) for value in (own, back, key_cosine, key_sine)],
                pltpu.VMEM((tokens, HEAD_DIM), jnp.bfloat16),
                tokens * HEAD_DIM * 8,
            )
            partner = swapped(own_kv, "tensor", 1)

    done, work = [], tokens * SEQ_LEN * HEAD_DIM * 4
    held = pltpu.VMEM((tokens, HEAD_DIM), jnp.bfloat16)
    for own, back in sums[1:-1]:
        operands = [near(value) for value in (own, back, cosine, sine, own_kv, partner)]
        done.append(call(head_kernel, [facts], operands, held, work))
    own, back = sums[-1]
    return call(
        head_kernel,
        [facts],
        [near(value) for value in (own, back, cosine, sine, own_kv, partner, *done)],
        jax.ShapeDtypeStruct((tokens, heads * HEAD_DIM), jnp.bfloat16),
        work,
        out_specs=pl.BlockSpec(memory_space=pltpu.HBM),
        scratch_shapes=[held, pltpu.SemaphoreType.DMA((len(done) + tokens // SEQ_LEN,))],
    )


def many_sections(hidden, q_weight, kv_weight, owner, lengths):
    rank, tensor_index = lax.axis_index("dp"), lax.axis_index("tensor")
    sections = lax.axis_size("dp") // OLD_DATA
    quarter, core = rank % OLD_DATA, tensor_index % 2
    keep = owner[quarter] == rank // OLD_DATA
    raw = jnp.concatenate([q_weight, kv_weight], axis=1)
    same = [[s * OLD_DATA + q for s in range(sections)] for q in range(OLD_DATA)]
    mine = lax.psum(jnp.where(keep, raw, jnp.zeros_like(raw)), "dp", axis_index_groups=same)
    group = [[s * OLD_DATA + q for q in range(OLD_DATA)] for s in range(sections)]
    weight = lax.all_gather(mine, "dp", axis_index_groups=group, tiled=True)
    q_width, tokens = q_weight.shape[1], hidden.shape[0]
    seqs = tokens // SEQ_LEN
    cosine, sine, key_cosine, key_sine = tables(core == 0)

    def turned(values, cosine, sine):
        shaped = values.reshape(seqs, SEQ_LEN, -1, HEAD_DIM // 2, 2)
        swapped = shaped[..., ::-1].reshape(seqs, SEQ_LEN, -1, HEAD_DIM)
        straight = values.reshape(seqs, SEQ_LEN, -1, HEAD_DIM)
        return (straight * cosine[:, None, :] + swapped * sine[:, None, :]).astype(jnp.bfloat16)

    queries = turned(dot(hidden, weight[:, :q_width]), cosine, sine)
    own = turned(dot(hidden, weight[:, q_width:]), key_cosine, key_sine)[:, :, 0]
    partner = swapped(own, "tensor", 1)
    keys = jnp.where(core == 0, own, partner)
    values = jnp.where(core == 0, partner, own)
    spots = jnp.arange(SEQ_LEN)
    allowed = (spots[None, None, :] <= spots[None, :, None]) & (spots[None, None, :] < lengths[:, None, None])
    scores = jnp.einsum("sqhd,skd->shqk", queries, keys, preferred_element_type=jnp.float32)
    scores = jnp.where(allowed[:, None], scores / math.sqrt(HEAD_DIM), -1e30)
    raised = jnp.exp(scores - jnp.max(scores, axis=-1, keepdims=True))
    probs = (raised / jnp.sum(raised, axis=-1, keepdims=True)).astype(jnp.bfloat16)
    mixed = jnp.einsum("shqk,skd->sqhd", probs, values, preferred_element_type=jnp.float32)
    return mixed.astype(jnp.bfloat16).reshape(tokens, q_width)


def body(hidden, q_weight, kv_weight, owner, lengths):
    if lax.axis_size("dp") == 2 * OLD_DATA:
        return two_sections(hidden, q_weight, kv_weight, owner, lengths)
    return many_sections(hidden, q_weight, kv_weight, owner, lengths)


def solution(mesh):
    return jax.shard_map(
        body,
        mesh=mesh,
        in_specs=(P("dp", None), P("dp", "tensor"), P("dp", "tensor"), P(), P("dp")),
        out_specs=P("dp", "tensor"),
        check_vma=False,
    )
```

```python
import functools
import math

import jax
import jax.numpy as jnp
from jax import lax
from jax.experimental import pallas as pl
from jax.experimental.pallas import tpu as pltpu
from jax.sharding import PartitionSpec as P


HEAD_DIM = 128
SEQ_LEN = 256
OLD_DATA = 4


VMEM = pl.BlockSpec(memory_space=pltpu.VMEM)
SMEM = pl.BlockSpec(memory_space=pltpu.SMEM)
ANY = pl.BlockSpec(memory_space=pl.ANY)


def swapped(value, axis, mask):
    pairs = [(source, source ^ mask) for source in range(lax.axis_size(axis))]
    return lax.ppermute(value, axis, pairs)


def near(value):
    return pltpu.with_memory_space_constraint(value, pltpu.VMEM)


def dot(left, right):
    return jnp.dot(left, right, preferred_element_type=jnp.float32)


def call(kernel, scalars, operands, outs, cost, out_specs=VMEM, **more):
    return pl.pallas_call(
        kernel,
        out_shape=outs,
        in_specs=[SMEM] * len(scalars) + [VMEM] * len(operands),
        out_specs=jax.tree.map(lambda _: out_specs, outs),
        compiler_params=pltpu.CompilerParams(vmem_limit_bytes=8 * 2**20),
        cost_estimate=pl.CostEstimate(flops=cost, bytes_accessed=cost // 256, transcendentals=0),
        **more,
    )(*scalars, *operands)


def tables(turned):
    columns = jnp.arange(HEAD_DIM)
    positions = jnp.arange(SEQ_LEN)
    pair_index = columns // 2
    inverse = jnp.exp(-(2.0 * pair_index.astype(jnp.float32) / HEAD_DIM) * math.log(10000.0))
    angles = positions.astype(jnp.float32)[:, None] * inverse[None, :]
    signs = jnp.where(columns % 2 == 0, -1.0, 1.0).astype(jnp.float32)
    cosine = jnp.cos(angles)
    sine = jnp.sin(angles) * signs[None, :]
    return cosine, sine, jnp.where(turned, cosine, 1.0), jnp.where(turned, sine, 0.0)


def turn(values, cosine, sine):
    lanes = lax.broadcasted_iota(jnp.int32, values.shape, 1)
    swapped = jnp.take_along_axis(values, lanes ^ 1, axis=1, mode="promise_in_bounds")
    return values * cosine + swapped * sine


def attend_head(queries, keys, values, length):
    half = SEQ_LEN // 2
    scale = math.log2(math.e) / math.sqrt(HEAD_DIM)
    values = jnp.concatenate([values, jnp.ones_like(values)], axis=1)
    every = lax.dot_general(
        queries, keys, (((1,), (1,)), ((), ())), preferred_element_type=jnp.float32
    )
    parts = []
    for start, stop in ((0, half), (half, SEQ_LEN)):
        rows = start + lax.broadcasted_iota(jnp.int32, (stop - start, stop), 0)
        spots = lax.broadcasted_iota(jnp.int32, (stop - start, stop), 1)
        scores = jnp.where((spots <= rows) & (spots < length), every[start:stop, :stop], -1e30)
        top = jnp.max(scores, axis=-1, keepdims=True)
        parts.append(jnp.exp2((scores - top) * scale).astype(jnp.bfloat16))
    parts[0] = jnp.concatenate([parts[0], jnp.zeros_like(parts[0])], axis=1)
    mixed = dot(jnp.concatenate(parts, axis=0), values)
    return mixed[:, :HEAD_DIM] / mixed[:, HEAD_DIM:]


def choose_kernel(keep_ref, raw_ref, other_ref, out_ref, sem):
    for kept, ref in ((1, raw_ref), (0, other_ref)):

        @pl.when(keep_ref[0] == kept)
        def _(ref=ref):
            copy = pltpu.make_async_copy(ref, out_ref, sem)
            copy.start()
            copy.wait()


def choose(keep, raw, other):
    return pl.pallas_call(
        choose_kernel,
        out_shape=pltpu.VMEM(raw.shape, raw.dtype),
        in_specs=[SMEM, ANY, ANY],
        out_specs=VMEM,
        scratch_shapes=[pltpu.SemaphoreType.DMA],
        compiler_params=pltpu.CompilerParams(vmem_limit_bytes=8 * 2**20),
        cost_estimate=pl.CostEstimate(flops=0, bytes_accessed=4 * raw.size, transcendentals=0),
    )(keep, raw, other)


def own_kernel(own_ref, mine_ref, far_ref, out_ref):
    depth = mine_ref.shape[0]
    out_ref[...] = dot(own_ref[:, :depth], mine_ref[...]) + dot(own_ref[:, depth:], far_ref[...])


def their_kernel(start, core_ref, first_ref, second_ref, block_ref, *refs):
    out_ref, half, depth = refs[-1], first_ref.shape[0], block_ref.shape[0]
    block = block_ref[...]
    for which, ref in ((core_ref[0], first_ref), (1 - core_ref[0], second_ref)):
        at = pl.ds(pl.multiple_of(which * half, half), half)
        total = dot(ref[:, start : start + depth], block)
        if len(refs) > 1:
            total += refs[0][at, :]
        out_ref[at, :] = total.astype(out_ref.dtype)


def finish_kernel(own_ref, sent_ref, cos_ref, sin_ref, out_ref):
    for seq in range(own_ref.shape[0] // SEQ_LEN):
        cut = slice(seq * SEQ_LEN, (seq + 1) * SEQ_LEN)
        total = own_ref[cut, :] + sent_ref[cut, :].astype(jnp.float32)
        out_ref[cut, :] = turn(total, cos_ref[...], sin_ref[...]).astype(out_ref.dtype)


def head_kernel(facts_ref, own_ref, sent_ref, cos_ref, sin_ref, kv_ref, partner_ref, *refs):
    seqs = own_ref.shape[0] // SEQ_LEN
    is_even = facts_ref[seqs] == 1
    last = len(refs) > 1
    done_refs, held = refs[:-3], refs[-2] if last else refs[0]
    copies = []

    def send(ref, head, cut):
        if last:
            columns = slice(head * HEAD_DIM, (head + 1) * HEAD_DIM)
            copy = pltpu.make_async_copy(ref.at[cut, :], refs[-3].at[cut, columns], refs[-1].at[len(copies)])
            copies.append(copy)
            copy.start()

    for head, ref in enumerate(done_refs):
        send(ref, head, slice(0, ref.shape[0]))
    for seq in range(seqs):
        cut = slice(seq * SEQ_LEN, (seq + 1) * SEQ_LEN)
        total = own_ref[cut, :] + sent_ref[cut, :].astype(jnp.float32)
        queries = turn(total, cos_ref[...], sin_ref[...]).astype(jnp.bfloat16)
        mine, partner = kv_ref[cut, :], partner_ref[cut, :]
        keys = jnp.where(is_even, mine, partner)
        values = jnp.where(is_even, partner, mine)
        held[cut, :] = attend_head(queries, keys, values, facts_ref[seq]).astype(held.dtype)
        send(held, len(done_refs), cut)
    for copy in copies:
        copy.wait()


def two_sections(hidden, q_weight, kv_weight, owner, lengths):
    rank, tensor_index = lax.axis_index("dp"), lax.axis_index("tensor")
    quarter, core = rank % OLD_DATA, tensor_index % 2
    keep = owner[quarter] == rank // OLD_DATA
    depth, tokens = q_weight.shape[0], hidden.shape[0]
    heads = q_weight.shape[1] // HEAD_DIM
    after = lax.optimization_barrier

    half = tokens // 2
    given = lambda w: lax.dynamic_slice(hidden, (core * half, w * depth), (half, depth))
    sent = jnp.concatenate([given(quarter ^ 1), given(quarter ^ 3)], axis=1)
    whole = lambda w: lax.dynamic_slice(hidden, (0, w * depth), (tokens, depth))
    own_part = jnp.concatenate([whole(quarter), whole(quarter ^ 2)], axis=1)
    first = swapped(sent, "dp", 1)

    columns = [q_weight[:, head * HEAD_DIM : (head + 1) * HEAD_DIM] for head in range(heads)]
    blocks = [kv_weight, *after(tuple(columns))]
    others = []
    for index, raw in enumerate(blocks):
        if index == 1:
            raw, staged = after((raw, choose(jnp.ones((1,), jnp.int32), kv_weight, kv_weight)))
            blocks[0] = staged
        if index:
            raw, others[0] = after((raw, others[0]))
        if index > 1:
            raw, own_part = after((raw, own_part))
        blocks[index] = raw
        others.append(swapped(raw, "dp", OLD_DATA))
    even = (core == 0).astype(jnp.int32).reshape(1)
    facts = jnp.concatenate([lengths, even])
    core = core.astype(jnp.int32).reshape(1)
    keep = keep.astype(jnp.int32).reshape(1)
    first, turns = after((first, tables(even[0] == 1)))
    cosine, sine, key_cosine, key_sine = turns
    second = swapped(first, "tensor", 1)
    settled = []
    for raw, other in zip(blocks, others):
        mine = choose(keep, raw, other)
        settled.append((mine, swapped(mine, "dp", 2)))

    sums, dots = [], 4 * tokens * depth * HEAD_DIM
    for index, (mine, far) in enumerate(settled):
        if index > 1:
            own, back = sums[-1]
            far, own = after((far, own))
            sums[-1] = (own, back)
        theirs = call(
            functools.partial(their_kernel, 0),
            [core],
            [near(value) for value in (first, second, mine)],
            pltpu.VMEM((tokens, HEAD_DIM), jnp.float32),
            dots // 2,
        )
        if index > 1:
            far, theirs = after((far, theirs))
        theirs = call(
            functools.partial(their_kernel, depth),
            [core],
            [near(value) for value in (first, second, far, theirs)],
            pltpu.VMEM((tokens, HEAD_DIM), jnp.float32 if index < 2 else jnp.bfloat16),
            dots // 2,
        )
        back = swapped(theirs, "dp", 1)
        own = call(
            own_kernel,
            [],
            [near(value) for value in (own_part, mine, far)],
            pltpu.VMEM((tokens, HEAD_DIM), jnp.float32),
            dots,
        )
        sums.append((own, back))
        if index == 0:
            own_kv = call(
                finish_kernel,
                [],
                [near(value) for value in (own, back, key_cosine, key_sine)],
                pltpu.VMEM((tokens, HEAD_DIM), jnp.bfloat16),
                tokens * HEAD_DIM * 8,
            )
            partner = swapped(own_kv, "tensor", 1)

    done, work = [], tokens * SEQ_LEN * HEAD_DIM * 4
    held = pltpu.VMEM((tokens, HEAD_DIM), jnp.bfloat16)
    for own, back in sums[1:-1]:
        operands = [near(value) for value in (own, back, cosine, sine, own_kv, partner)]
        done.append(call(head_kernel, [facts], operands, held, work))
    own, back = sums[-1]
    return call(
        head_kernel,
        [facts],
        [near(value) for value in (own, back, cosine, sine, own_kv, partner, *done)],
        jax.ShapeDtypeStruct((tokens, heads * HEAD_DIM), jnp.bfloat16),
        work,
        out_specs=pl.BlockSpec(memory_space=pltpu.HBM),
        scratch_shapes=[held, pltpu.SemaphoreType.DMA((len(done) + tokens // SEQ_LEN,))],
    )


def many_sections(hidden, q_weight, kv_weight, owner, lengths):
    rank, tensor_index = lax.axis_index("dp"), lax.axis_index("tensor")
    sections = lax.axis_size("dp") // OLD_DATA
    quarter, core = rank % OLD_DATA, tensor_index % 2
    keep = owner[quarter] == rank // OLD_DATA
    raw = jnp.concatenate([q_weight, kv_weight], axis=1)
    same = [[s * OLD_DATA + q for s in range(sections)] for q in range(OLD_DATA)]
    mine = lax.psum(jnp.where(keep, raw, jnp.zeros_like(raw)), "dp", axis_index_groups=same)
    group = [[s * OLD_DATA + q for q in range(OLD_DATA)] for s in range(sections)]
    weight = lax.all_gather(mine, "dp", axis_index_groups=group, tiled=True)
    q_width, tokens = q_weight.shape[1], hidden.shape[0]
    seqs = tokens // SEQ_LEN
    cosine, sine, key_cosine, key_sine = tables(core == 0)

    def turned(values, cosine, sine):
        shaped = values.reshape(seqs, SEQ_LEN, -1, HEAD_DIM // 2, 2)
        swapped = shaped[..., ::-1].reshape(seqs, SEQ_LEN, -1, HEAD_DIM)
        straight = values.reshape(seqs, SEQ_LEN, -1, HEAD_DIM)
        return (straight * cosine[:, None, :] + swapped * sine[:, None, :]).astype(jnp.bfloat16)

    queries = turned(dot(hidden, weight[:, :q_width]), cosine, sine)
    own = turned(dot(hidden, weight[:, q_width:]), key_cosine, key_sine)[:, :, 0]
    partner = swapped(own, "tensor", 1)
    keys = jnp.where(core == 0, own, partner)
    values = jnp.where(core == 0, partner, own)
    spots = jnp.arange(SEQ_LEN)
    allowed = (spots[None, None, :] <= spots[None, :, None]) & (spots[None, None, :] < lengths[:, None, None])
    scores = jnp.einsum("sqhd,skd->shqk", queries, keys, preferred_element_type=jnp.float32)
    scores = jnp.where(allowed[:, None], scores / math.sqrt(HEAD_DIM), -1e30)
    raised = jnp.exp(scores - jnp.max(scores, axis=-1, keepdims=True))
    probs = (raised / jnp.sum(raised, axis=-1, keepdims=True)).astype(jnp.bfloat16)
    mixed = jnp.einsum("shqk,skd->sqhd", probs, values, preferred_element_type=jnp.float32)
    return mixed.astype(jnp.bfloat16).reshape(tokens, q_width)


def body(hidden, q_weight, kv_weight, owner, lengths):
    if lax.axis_size("dp") == 2 * OLD_DATA:
        return two_sections(hidden, q_weight, kv_weight, owner, lengths)
    return many_sections(hidden, q_weight, kv_weight, owner, lengths)


def solution(mesh):
    return jax.shard_map(
        body,
        mesh=mesh,
        in_specs=(P("dp", None), P("dp", "tensor"), P("dp", "tensor"), P(), P("dp")),
        out_specs=P("dp", "tensor"),
        check_vma=False,
    )
```
